256 devices in a mesh: cfg: 2 (over core), seq: 64 (over x, z_hi, y), rep: 2 (over z_lo).
Axes of the slice: x: 4, y: 4, z: 8 (z_hi: 4, z_lo: 2; z = z_hi * 2 + z_lo), core: 2. Of those that a mesh axis runs over, the one named last changes fastest.
Arguments:
- queries: bfloat16 [2, 8192, 1536], P('cfg', 'seq', 'rep'), may hold values from -205 to 205
- keyvals: bfloat16 [2, 2, 8192, 1536], P('cfg', None, 'seq', 'rep'), may hold values from -13.5 to 13.5
- out_weight: bfloat16 [1536, 3072], P('rep', 'seq'), may hold values from -0.15625 to 0.15625
- latent: bfloat16 [8192, 3072], P('seq', ('cfg', 'rep')), may hold values from -6 to 6
- timestep: int32 [8192], P('seq'), may hold values from 0 to 49
- cond_mask: int32 [8192], P('seq'), may hold values 0 or 1
Outputs:
- denoised: bfloat16 [8192, 3072], P('seq', ('cfg', 'rep'))
The draws below stay inside these ranges and needn't reach their ends.
All inputs are finite; a program needn't handle non-finite values. No bound on the sum of `cond_mask` on one device may be relied on, other than what follows from the above.
Results may differ from the reference program's by a relative error of at most 0.012.
Values may be sent and summed in bfloat16 or wider, within the bound.
A program may use at most 128 MiB of HBM per device.

```python
import math
import jax
import jax.numpy as jnp
from jax import lax

D = 3072
HEADS = 12
HD = 128
NSTEPS = 50
FRAMES = 8192
HH = 1536


def common_draw(key):
    query_key = jax.random.fold_in(key, 101)
    keyval_key = jax.random.fold_in(key, 202)
    keyval_raw = jnp.clip(jax.random.normal(keyval_key, (2, 2, FRAMES, HH), jnp.float32), -4.5, 4.5)
    keyval_raw = keyval_raw * jnp.array([1.0, 3.0], jnp.float32)[None, :, None, None]
    query_raw = 2.0 * jnp.clip(jax.random.normal(query_key, (2, FRAMES, HH), jnp.float32), -4.5, 4.5)
    return (query_raw, keyval_raw)


def draw_queries(key, part):
    query_raw, keyval_raw = common_draw(key)
    return query_raw.astype(jnp.bfloat16)


def draw_keyvals(key, part):
    query_raw, keyval_raw = common_draw(key)
    return keyval_raw.astype(jnp.bfloat16)


def with_ends(values, rng, least, high):
    extent = values.shape
    spot = [jax.random.randint(jax.random.fold_in(rng, axis), (), 0, extent[axis]) for axis in range(len(extent))]
    values = values.at[tuple(spot)].set(least)
    longest = extent.index(max(extent))
    spot[longest] = (spot[longest] + 1) % extent[longest]
    return values.at[tuple(spot)].set(high)


def shard_levels(stream_key, extent, pieces, low, largest):
    factor_of, own = 1.0, jax.random.fold_in(stream_key, 6)
    for axis_at, shards_of in pieces:
        heights = jnp.exp(jax.random.uniform(jax.random.fold_in(own, axis_at), (shards_of,), jnp.float32, low / len(pieces), largest / len(pieces)))
        factor_of = factor_of * jnp.repeat(heights, extent[axis_at] // shards_of).reshape([-1 if axis == axis_at else 1 for axis in range(len(extent))])
    return factor_of


def scatter_about(rng, shape, deviation, bound, cuts=(), held_as=jnp.bfloat16):
    result = deviation * jax.random.normal(rng, shape, jnp.float32)
    if cuts:
        result = result * shard_levels(rng, shape, cuts, -0.22, 0.18)
    return jnp.clip(result, -bound, bound).astype(held_as)


def setup_inputs(seed: int = 0) -> dict:
    streams_of = jax.random.split(jax.random.key(seed), 7)
    return {
        "queries": draw_queries(jax.random.fold_in(streams_of[6], 71), 0),
        "keyvals": draw_keyvals(jax.random.fold_in(streams_of[6], 71), 0),
        "out_weight": scatter_about(streams_of[2], (HH, D), HH ** -0.5, 0.15625, ((0, 2), (1, 64))),
        "latent": scatter_about(streams_of[3], (FRAMES, D), 1.0, 6.0, ((0, 64), (1, 4))),
        "timestep": with_ends(jax.random.randint(streams_of[4], (FRAMES,), 0, NSTEPS), jax.random.fold_in(streams_of[4], 1), 0, NSTEPS - 1).astype(jnp.int32),
        "cond_mask": with_ends((jax.random.randint(streams_of[5], (FRAMES,), 0, 2) < 1).astype(jnp.int32), jax.random.fold_in(streams_of[5], 1), 0, 1),
    }


guide_scale = 3.0

def attend(query_rows, keyval_rows):
    block = math.gcd(FRAMES, 512)
    keys = keyval_rows[0].astype(jnp.float32).reshape(FRAMES, HEADS, HD)
    values = keyval_rows[1].astype(jnp.float32).reshape(FRAMES, HEADS, HD)
    blocks = query_rows.reshape(FRAMES // block, block, HEADS, HD)

    def one_block(query_block):
        scores = jnp.einsum('rhd,khd->hrk', query_block.astype(jnp.float32), keys) / math.sqrt(HD)
        top = lax.optimization_barrier(jnp.max(scores, axis=-1, keepdims=True))
        weights = jnp.exp(scores - top)
        total = lax.optimization_barrier(jnp.sum(weights, axis=-1))
        rounded = lax.optimization_barrier(weights.astype(jnp.bfloat16))
        mixed = jnp.einsum('hrk,khd->rhd', rounded.astype(jnp.float32), values)
        mixed = mixed / jnp.transpose(total)[:, :, None]
        return mixed.reshape(block, HH)
    return lax.map(one_block, blocks).reshape(FRAMES, HH).astype(jnp.bfloat16)

def reference(queries, keyvals, out_weight, latent, timestep, cond_mask):
    cond_out = jnp.dot(attend(queries[0], keyvals[0]), out_weight, preferred_element_type=jnp.float32)
    uncond_out = jnp.dot(attend(queries[1], keyvals[1]), out_weight, preferred_element_type=jnp.float32)
    factor = 1.0 + (guide_scale - 1.0) * cond_mask.astype(jnp.float32)
    guided = factor[:, None] * cond_out + (1.0 - factor)[:, None] * uncond_out
    sigma = 0.5 * jnp.exp(math.log(8.0) * timestep.astype(jnp.float32) / (NSTEPS - 1))
    return (latent.astype(jnp.float32) - sigma[:, None] * guided).astype(jnp.bfloat16)
```

```python
import math

import jax
import jax.numpy as jnp
from jax import lax
from jax.experimental import pallas as pl
from jax.experimental.pallas import tpu as pltpu
from jax.sharding import PartitionSpec as P

HD = 128
NSTEPS = 50
guide_scale = 3.0
SCALE = math.log2(math.e) / math.sqrt(HD)
MESH = pl.DeviceIdType.MESH
F32 = jnp.float32
BF16 = jnp.bfloat16


def dot_t(a, b):
    return lax.dot_general(a, b, (((1,), (1,)), ((), ())), preferred_element_type=F32)


def rcopy(src, dst, send_sem, recv_sem, device):
    return pltpu.make_async_remote_copy(
        src_ref=src, dst_ref=dst, send_sem=send_sem, recv_sem=recv_sem,
        device_id=device, device_id_type=MESH,
    )


def kernel(q_in, kv_in, w_in, mask_in, out_ref,
           kv, qb, osend, opart, lsend, lpart, ored, oz, cmb, wt, wb,
           sz, sy, ss, sx, so, sl, sr, sc, sw,
           rt, rq, ry, rs, rx, ro, rl, rz, rc, rwa, rw):
    c = lax.axis_index("cfg")
    s = lax.axis_index("seq")
    r = lax.axis_index("rep")
    x, k, y = s // 16, (s // 4) % 4, s % 4

    def dev(c_, x_, k_, y_, r_):
        return (c_, x_ * 16 + k_ * 4 + y_, r_)

    def xdev(d):
        return dev(c, (x + d) % 4, k, y, r)

    def ydev(d):
        return dev(c, x, k, (y + d) % 4, r)

    def zdev(d):
        return dev(c, x, (k + d) % 4, y, r)

    wdx, wsx = 2 * r + c, 2 * c + r
    wdest = dev(x // 2, wdx, k, y, x % 2)
    wsrc = dev(x % 2, wsx, k, y, x // 2)
    wself = jnp.logical_and(jnp.logical_and(wdx == x, x // 2 == c), x % 2 == r)

    barrier = pltpu.get_barrier_semaphore()

    def hello(device):
        pl.semaphore_signal(barrier, inc=1, device_id=device, device_id_type=MESH)

    for d in range(1, 4):
        hello(xdev(d))
        hello(ydev(d))
        hello(zdev(d))
    for d in range(4):
        hello(dev(1 - c, x, (k + d) % 4, y, r))
    hello(dev(c, x, k, y, 1 - r))
    hello(dev(1 - c, x, k, y, 1 - r))

    @pl.when(jnp.logical_not(wself))
    def _():
        hello(wdest)
        hello(wsrc)

    eye48 = jnp.where(
        lax.broadcasted_iota(jnp.int32, (48, 48), 0) == lax.broadcasted_iota(jnp.int32, (48, 48), 1), 1.0, 0.0
    ).astype(BF16)
    wt[...] = dot_t(eye48, w_in[...]).astype(BF16)
    eye = lax.broadcasted_iota(jnp.int32, (128, 128), 0) == lax.broadcasted_iota(jnp.int32, (128, 128), 1)

    def to_row(col):
        return jnp.sum(jnp.where(eye, jnp.broadcast_to(col, (128, 128)), 0.0), axis=0, keepdims=True)

    def to_col(row):
        return jnp.sum(jnp.where(eye, jnp.broadcast_to(row, (128, 128)), 0.0), axis=1, keepdims=True)

    pl.semaphore_wait(barrier, jnp.where(wself, 15, 17))

    def z_copies(j, q, t):
        kd = 2 * c + q
        lanes = pl.ds(384 * q + 128 * j, 128)
        if t == 2:
            core = k // 2
            return (q_in.at[:, lanes], qb.at[j, x, k % 2], rq.at[j], core, kd, kd == k)
        return (kv_in.at[t, :, lanes], kv.at[t, j, y, k], rt.at[j], t, kd, jnp.logical_and(kd == k, c == t))

    def z_remote(j, q, t):
        src, dst, sem, core, kd, same = z_copies(j, q, t)
        return rcopy(src, dst, sz.at[j, q, t], sem, dev(core, x, kd, y, r)), src, dst, sem, same

    for j in range(3):
        for t in (2, 0, 1):
            for q in range(2):
                copy, src, dst, sem, same = z_remote(j, q, t)

                @pl.when(same)
                def _():
                    pltpu.make_async_copy(src, dst, sem).start()

                @pl.when(jnp.logical_not(same))
                def _():
                    copy.start()

    wcopy = rcopy(wt.at[:, pl.ds(pl.multiple_of(384 * c, 128), 384)],
                  wb.at[k, y, :, pl.ds(pl.multiple_of(384 * wdx, 128), 384)], sw.at[0], rwa, wdest)
    my_lanes = pl.ds(pl.multiple_of(384 * x, 128), 384)

    @pl.when(wself)
    def _():
        pltpu.make_async_copy(wt.at[:, pl.ds(pl.multiple_of(384 * c, 128), 384)],
                              wb.at[k, y, :, my_lanes], rwa).start()

    @pl.when(jnp.logical_not(wself))
    def _():
        wcopy.start()

    def x_copy(j, d):
        return rcopy(qb.at[j, x], qb.at[j, x], sx.at[j, d], rx.at[j, d], xdev(d))

    def x_wait(j, d):
        src = (x + 4 - d) % 4
        rcopy(qb.at[j, src], qb.at[j, src], sx.at[j, d], rx.at[j, d], xdev(d)).wait_recv()

    def y_copy(j, d):
        return rcopy(kv.at[c, j, y], kv.at[c, j, y], sy.at[j, d], ry.at[j, d], ydev(d))

    def y_wait(j, d):
        src = (y + 4 - d) % 4
        rcopy(kv.at[c, j, src], kv.at[c, j, src], sy.at[j, d], ry.at[j, d], ydev(d)).wait_recv()

    def s_copy(j, d):
        src = (y + 4 - d) % 4
        return rcopy(kv.at[c, j, src], kv.at[c, j, src], ss.at[j, d], rs.at[j, d], dev(1 - c, x, k, y, r))

    def s_wait(j, d):
        src = (y + 4 - d) % 4
        rcopy(kv.at[1 - c, j, src], kv.at[1 - c, j, src], ss.at[j, d], rs.at[j, d],
              dev(1 - c, x, k, y, r)).wait_recv()

    def relay(j):
        rcopy(qb.at[j, x], qb.at[j, x], sx.at[j, 0], rq.at[j], xdev(1)).wait_recv()
        for d in (1, 3, 2):
            x_copy(j, d).start()
        rcopy(kv.at[c, j, y], kv.at[c, j, y], sx.at[j, 0], rt.at[j], ydev(1)).wait_recv()
        for d in (1, 3, 2):
            y_copy(j, d).start()
        s_copy(j, 0).start()

    def share(j):
        for d in (1, 3, 2):
            y_wait(j, d)
            s_copy(j, d).start()

    lo, hi = pl.ds(0, 2), pl.ds(2, 2)

    def wz(d):
        return rcopy(wb.at[k, y, :, my_lanes], wb.at[k, y, :, my_lanes], sw.at[d], rw.at[0, d], zdev(d))

    def wz_wait(d):
        kk = (k + 4 - d) % 4
        rcopy(wb.at[kk, y, :, my_lanes], wb.at[kk, y, :, my_lanes], sw.at[d], rw.at[0, d], zdev(d)).wait_recv()

    def lanes_of(xx):
        return pl.ds(pl.multiple_of(384 * xx, 128), 384)

    def wa2(d, yy):
        return rcopy(wb.at[lo, yy, :, my_lanes], wb.at[lo, yy, :, my_lanes], sw.at[3 + d], rw.at[1, d], ydev(d))

    def wb2(d, xx):
        return rcopy(wb.at[hi, y, :, lanes_of(xx)], wb.at[hi, y, :, lanes_of(xx)], sw.at[6 + d], rw.at[2, d], xdev(d))

    def wa3(d, xx):
        return rcopy(wb.at[lo, :, :, lanes_of(xx)], wb.at[lo, :, :, lanes_of(xx)], sw.at[9 + d], rw.at[3, d], xdev(d))

    def wb3(d, yy):
        return rcopy(wb.at[hi, yy], wb.at[hi, yy], sw.at[12 + d], rw.at[4, d], ydev(d))

    def w_first():
        rcopy(wb.at[k, y, :, my_lanes], wb.at[k, y, :, my_lanes], sw.at[0], rwa, wdest).wait_recv()
        for d in (1, 3, 2):
            wz(d).start()

    def w_second():
        for d in (1, 3, 2):
            wz_wait(d)
        for d in (1, 3, 2):
            wa2(d, y).start()
            wb2(d, x).start()

    def w_third():
        for d in (1, 3, 2):
            wa2(d, (y + 4 - d) % 4).wait_recv()
            wb2(d, (x + 4 - d) % 4).wait_recv()
        for d in (1, 3, 2):
            wa3(d, x).start()
            wb3(d, y).start()

    def w_last():
        for d in (1, 3, 2):
            wa3(d, (x + 4 - d) % 4).wait_recv()
            wb3(d, (y + 4 - d) % 4).wait_recv()

    def o_copy(j, d):
        return rcopy(osend.at[j, d], opart.at[j, d], so.at[j, d], ro.at[j, d], xdev(4 - d))

    def l_copy(j, d):
        return rcopy(lsend.at[j, d], lpart.at[j, d], sl.at[j, d], rl.at[j, d], xdev(4 - d))

    def compute(j):
        for d in range(4):
            s_wait(j, d)
        for d in range(1, 4):
            x_wait(j, d)

        def tile(d):
            qq = qb[j, (x + 4 - d) % 4].reshape(256, HD)
            scores = dot_t(qq, kv[0, j].reshape(2048, HD))
            top = jnp.max(scores, axis=1, keepdims=True)
            weights = jnp.exp2((scores - top) * SCALE)
            total = jnp.sum(weights, axis=1, keepdims=True)
            mixed = jnp.dot(weights.astype(BF16), kv[1, j].reshape(2048, HD), preferred_element_type=F32)
            osend[j, d] = (mixed * (1.0 / total)).astype(BF16)
            level = top * SCALE + jnp.log2(total)
            lsend[j, d] = jnp.concatenate(
                [jnp.broadcast_to(to_row(level[:128]), (4, 128)), jnp.broadcast_to(to_row(level[128:]), (4, 128))],
                axis=0,
            )

        def pair(u, carry):
            d0, d1 = 2 * u + 1, (2 * u + 2) % 4
            tile(d0)
            tile(d1)
            o_copy(j, d0).start()
            l_copy(j, d0).start()

            @pl.when(u == 0)
            def _():
                o_copy(j, d1).start()
                l_copy(j, d1).start()

            return carry

        lax.fori_loop(0, 2, pair, 0)

    oq = k % 2
    ob = k // 2

    def r_copy(j, h):
        return rcopy(ored.at[j, h], oz.at[ob, j], sr.at[j, h], rz.at[ob, j], dev(oq, x, 2 * c + h, y, r))

    def r_same(h):
        return jnp.logical_and(2 * c + h == k, oq == c)

    def merge(j):
        for d in range(1, 4):
            o_copy(j, d).wait_recv()
            l_copy(j, d).wait_recv()
        levels = [lsend[j, 0]] + [lpart[j, d] for d in range(1, 4)]
        best = jnp.maximum(jnp.maximum(levels[0], levels[1]), jnp.maximum(levels[2], levels[3]))
        parts = [jnp.exp2(v - best) for v in levels]
        inv = 1.0 / (parts[0] + parts[1] + parts[2] + parts[3])
        for h in range(2):
            total = None
            for d in range(4):
                share_d = to_col((parts[d] * inv)[4 * h:4 * h + 1])
                rows = pl.ds(128 * h, 128)
                block = osend[j, 0, rows, :] if d == 0 else opart[j, d, rows, :]
                term = block.astype(F32) * share_d
                total = term if total is None else total + term
            ored[j, h] = total.astype(BF16)
        for h in range(2):
            @pl.when(r_same(h))
            def _():
                pltpu.make_async_copy(ored.at[j, h], oz.at[ob, j], rz.at[ob, j]).start()

            @pl.when(jnp.logical_not(r_same(h)))
            def _():
                r_copy(j, h).start()

    factor = 1.0 + (guide_scale - 1.0) * to_col(mask_in[...].astype(F32))

    def c_lanes(rr, qq, j):
        return pl.ds(pl.multiple_of(128 * (6 * rr + 3 * qq + j), 128), 128)

    def c_peer(n):
        return (c if n == 1 else 1 - c), (r if n == 0 else 1 - r)

    def c_copy(j, n):
        cc, rr = c_peer(n)
        lanes = c_lanes(r, c, j)
        return rcopy(cmb.at[:, lanes], cmb.at[:, lanes], sc.at[j, n], rc.at[j, n], dev(cc, x, k, y, rr))

    def c_wait(j, n):
        cc, rr = c_peer(n)
        lanes = c_lanes(rr, cc, j)
        rcopy(cmb.at[:, lanes], cmb.at[:, lanes], sc.at[j, n], rc.at[j, n], dev(cc, x, k, y, rr)).wait_recv()

    def combine(j):
        for b in range(2):
            rcopy(oz.at[b, j], oz.at[b, j], sr.at[j, 0], rz.at[b, j], dev(1 - c, x, k, y, r)).wait_recv()
        guided = factor * oz[0, j].astype(F32) + (1.0 - factor) * oz[1, j].astype(F32)
        cmb[:, c_lanes(r, c, j)] = guided.astype(BF16)
        for n in (1, 2, 0):
            c_copy(j, n).start()

    relay(0)
    w_first()
    relay(1)
    share(0)
    relay(2)
    compute(0)
    share(1)
    w_second()
    compute(1)
    merge(0)
    share(2)
    w_third()
    compute(2)
    combine(0)
    merge(1)
    combine(1)
    merge(2)
    combine(2)
    for j in range(3):
        for n in range(3):
            c_wait(j, n)
    w_last()
    out_ref[...] = dot_t(cmb[...], wb[...].reshape(768, 1536))

    for j in range(3):
        for q in range(2):
            for t in range(3):
                copy, _src, _dst, _sem, same = z_remote(j, q, t)

                @pl.when(jnp.logical_not(same))
                def _():
                    copy.wait_send()

        for d in range(1, 4):
            x_copy(j, d).wait_send()
            y_copy(j, d).wait_send()
            o_copy(j, d).wait_send()
            l_copy(j, d).wait_send()
        for d in range(4):
            s_copy(j, d).wait_send()
        for h in range(2):
            @pl.when(jnp.logical_not(r_same(h)))
            def _():
                r_copy(j, h).wait_send()

        for n in range(3):
            c_copy(j, n).wait_send()

    @pl.when(jnp.logical_not(wself))
    def _():
        wcopy.wait_send()

    for d in range(1, 4):
        wz(d).wait_send()
        wa2(d, y).wait_send()
        wb2(d, x).wait_send()
        wa3(d, x).wait_send()
        wb3(d, y).wait_send()


def on_device(queries, keyvals, out_weight, latent, timestep, cond_mask):
    rows = queries.shape[1]
    dma = pltpu.SemaphoreType.DMA
    vmem = pltpu.VMEM
    guided = pl.pallas_call(
        kernel,
        out_shape=jax.ShapeDtypeStruct((rows, 768), F32),
        in_specs=[pl.BlockSpec(memory_space=vmem)] * 4,
        out_specs=pl.BlockSpec(memory_space=vmem),
        scratch_shapes=[
            vmem((2, 3, 4, 4, 128, HD), BF16),
            vmem((3, 4, 2, 128, HD), BF16),
            vmem((3, 4, 256, HD), BF16),
            vmem((3, 4, 256, HD), BF16),
            vmem((3, 4, 8, 128), F32),
            vmem((3, 4, 8, 128), F32),
            vmem((3, 2, 128, HD), BF16),
            vmem((2, 3, 128, HD), BF16),
            vmem((128, 1536), BF16),
            vmem((48, 768), BF16),
            vmem((4, 4, 48, 1536), BF16),
            dma((3, 2, 3)), dma((3, 4)), dma((3, 4)), dma((3, 4)), dma((3, 4)), dma((3, 4)),
            dma((3, 2)), dma((3, 3)), dma((16,)),
            dma((3,)), dma((3,)), dma((3, 4)), dma((3, 4)), dma((3, 4)), dma((3, 4)), dma((3, 4)),
            dma((2, 3)), dma((3, 3)), dma, dma((5, 4)),
        ],
        compiler_params=pltpu.CompilerParams(
            collective_id=0, has_side_effects=True, vmem_limit_bytes=58 << 20
        ),
    )(queries[0], keyvals[0], out_weight, cond_mask.reshape(1, rows))
    sigma = 0.5 * jnp.exp(math.log(8.0) * timestep.astype(F32) / (NSTEPS - 1))
    return (latent.astype(F32) - sigma[:, None] * guided).astype(BF16)


def solution(mesh):
    placed = (
        P("cfg", "seq", "rep"),
        P("cfg", None, "seq", "rep"),
        P("rep", "seq"),
        P("seq", ("cfg", "rep")),
        P("seq"),
        P("seq"),
    )
    return jax.shard_map(
        on_device, mesh=mesh, in_specs=placed, out_specs=P("seq", ("cfg", "rep")), check_vma=False
    )
```

```python
import math

import jax
import jax.numpy as jnp
from jax import lax
from jax.experimental import pallas as pl
from jax.experimental.pallas import tpu as pltpu
from jax.sharding import PartitionSpec as P

HD = 128
NSTEPS = 50
guide_scale = 3.0
SCALE = math.log2(math.e) / math.sqrt(HD)
MESH = pl.DeviceIdType.MESH
F32 = jnp.float32
BF16 = jnp.bfloat16


def dot_t(a, b):
    return lax.dot_general(a, b, (((1,), (1,)), ((), ())), preferred_element_type=F32)


def rcopy(src, dst, send_sem, recv_sem, device):
    return pltpu.make_async_remote_copy(
        src_ref=src, dst_ref=dst, send_sem=send_sem, recv_sem=recv_sem,
        device_id=device, device_id_type=MESH,
    )


def kernel(q_hbm, kv_hbm, w_hbm, latent_hbm, step_in, mask_in, out_ref,
           q_in, kv_in, wt, lat, kv, qb, osend, opart, lsend, lpart, ored, oz, cmb, wb,
           sz, sy, ss, sx, so, sl, sr, sc, sw,
           rt, rq, ry, rs, rx, ro, rl, rz, rc, rwa, rw, sin):
    c = lax.axis_index("cfg")
    s = lax.axis_index("seq")
    r = lax.axis_index("rep")
    x, k, y = s // 16, (s // 4) % 4, s % 4

    def dev(c_, x_, k_, y_, r_):
        return (c_, x_ * 16 + k_ * 4 + y_, r_)

    def xdev(d):
        return dev(c, (x + d) % 4, k, y, r)

    def ydev(d):
        return dev(c, x, k, (y + d) % 4, r)

    def zdev(d):
        return dev(c, x, (k + d) % 4, y, r)

    wdx, wsx = 2 * r + c, 2 * c + r
    wdest = dev(x // 2, wdx, k, y, x % 2)
    wsrc = dev(x % 2, wsx, k, y, x // 2)
    wself = jnp.logical_and(jnp.logical_and(wdx == x, x // 2 == c), x % 2 == r)

    barrier = pltpu.get_barrier_semaphore()

    def hello(device):
        pl.semaphore_signal(barrier, inc=1, device_id=device, device_id_type=MESH)

    for d in range(1, 4):
        hello(xdev(d))
        hello(ydev(d))
        hello(zdev(d))
    for d in range(4):
        hello(dev(1 - c, x, (k + d) % 4, y, r))
    hello(dev(c, x, k, y, 1 - r))
    hello(dev(1 - c, x, k, y, 1 - r))

    @pl.when(jnp.logical_not(wself))
    def _():
        hello(wdest)
        hello(wsrc)

    staged = [
        pltpu.make_async_copy(src, dst, sin.at[n])
        for n, (src, dst) in enumerate(((q_hbm, q_in), (kv_hbm, kv_in), (w_hbm, wt), (latent_hbm, lat)))
    ]
    for copy in staged:
        copy.start()
    eye = lax.broadcasted_iota(jnp.int32, (128, 128), 0) == lax.broadcasted_iota(jnp.int32, (128, 128), 1)

    def to_row(col):
        return jnp.sum(jnp.where(eye, jnp.broadcast_to(col, (128, 128)), 0.0), axis=0, keepdims=True)

    def to_col(row):
        return jnp.sum(jnp.where(eye, jnp.broadcast_to(row, (128, 128)), 0.0), axis=1, keepdims=True)

    for copy in staged:
        copy.wait()
    pl.semaphore_wait(barrier, jnp.where(wself, 15, 17))

    def row_axis(j):
        return (y, ydev) if j == 1 else (x, xdev)

    def key_axis(j):
        return (x, xdev) if j == 1 else (y, ydev)

    def z_copies(j, q, t):
        kd = 2 * c + q
        lanes = pl.ds(384 * q + 128 * j, 128)
        if t == 2:
            core = k // 2
            return (q_in.at[:, lanes], qb.at[j, row_axis(j)[0], k % 2], rq.at[j], core, kd, kd == k)
        return (kv_in.at[t, :, lanes], kv.at[t, j, key_axis(j)[0], k], rt.at[j], t, kd, jnp.logical_and(kd == k, c == t))

    def z_remote(j, q, t):
        src, dst, sem, core, kd, same = z_copies(j, q, t)
        return rcopy(src, dst, sz.at[j, q, t], sem, dev(core, x, kd, y, r)), src, dst, sem, same

    for j in range(3):
        for t in (2, 0, 1):
            for q in range(2):
                copy, src, dst, sem, same = z_remote(j, q, t)

                @pl.when(same)
                def _():
                    pltpu.make_async_copy(src, dst, sem).start()

                @pl.when(jnp.logical_not(same))
                def _():
                    copy.start()

    wcopy = rcopy(wt.at[:, pl.ds(pl.multiple_of(384 * c, 128), 384)],
                  wb.at[wdx, k, y], sw.at[0], rwa, wdest)

    @pl.when(wself)
    def _():
        pltpu.make_async_copy(wt.at[:, pl.ds(pl.multiple_of(384 * c, 128), 384)],
                              wb.at[x, k, y], rwa).start()

    @pl.when(jnp.logical_not(wself))
    def _():
        wcopy.start()

    near = 1 + 2 * c

    def x_copy(j, d, src, to):
        block = qb.at[j, src]
        return rcopy(block, block, sx.at[j, d], rx.at[j, d], row_axis(j)[1](to))

    def x_send(j, d):
        return x_copy(j, d, row_axis(j)[0], d)

    def x_pass(j):
        return x_copy(j, 2, (row_axis(j)[0] + 4 - near) % 4, near)

    def x_wait(j, d):
        x_copy(j, d, (row_axis(j)[0] + 4 - d) % 4, d).wait_recv()

    def y_copy(j, d, src, to):
        block = kv.at[c, j, src]
        return rcopy(block, block, sy.at[j, d], ry.at[j, d], key_axis(j)[1](to))

    def y_send(j, d):
        return y_copy(j, d, key_axis(j)[0], d)

    def y_pass(j):
        return y_copy(j, 2, (key_axis(j)[0] + 4 - near) % 4, near)

    def y_wait(j, d):
        y_copy(j, d, (key_axis(j)[0] + 4 - d) % 4, d).wait_recv()

    def s_copy(j, d):
        block = kv.at[c, j, (key_axis(j)[0] + 4 - d) % 4]
        return rcopy(block, block, ss.at[j, d], rs.at[j, d], dev(1 - c, x, k, y, r))

    def s_wait(j, d):
        block = kv.at[1 - c, j, (key_axis(j)[0] + 4 - d) % 4]
        rcopy(block, block, ss.at[j, d], rs.at[j, d], dev(1 - c, x, k, y, r)).wait_recv()

    def relay(j):
        own = qb.at[j, row_axis(j)[0]]
        rcopy(own, own, sx.at[j, 0], rq.at[j], xdev(1)).wait_recv()
        for d in (1, 3):
            x_send(j, d).start()
        own = kv.at[c, j, key_axis(j)[0]]
        rcopy(own, own, sx.at[j, 0], rt.at[j], ydev(1)).wait_recv()
        for d in (1, 3):
            y_send(j, d).start()
        s_copy(j, 0).start()

    def forward(j):
        x_wait(j, near)
        x_pass(j).start()
        y_wait(j, near)
        y_pass(j).start()
        s_copy(j, near).start()
        y_wait(j, 4 - near)
        s_copy(j, 4 - near).start()

    def share(j):
        y_wait(j, 2)
        s_copy(j, 2).start()

    lo, hi = pl.ds(0, 2), pl.ds(2, 2)

    def wz(d):
        return rcopy(wb.at[x, k, y], wb.at[x, k, y], sw.at[d], rw.at[0, d], zdev(d))

    def wz_wait(d):
        kk = (k + 4 - d) % 4
        rcopy(wb.at[x, kk, y], wb.at[x, kk, y], sw.at[d], rw.at[0, d], zdev(d)).wait_recv()

    def wa2(d, yy):
        return rcopy(wb.at[x, lo, yy], wb.at[x, lo, yy], sw.at[3 + d], rw.at[1, d], ydev(d))

    def wb2(d, xx):
        return rcopy(wb.at[xx, hi, y], wb.at[xx, hi, y], sw.at[6 + d], rw.at[2, d], xdev(d))

    def wa3(d, xx):
        return rcopy(wb.at[xx, lo], wb.at[xx, lo], sw.at[9 + d], rw.at[3, d], xdev(d))

    def wb3(d, yy):
        return rcopy(wb.at[:, hi, yy], wb.at[:, hi, yy], sw.at[12 + d], rw.at[4, d], ydev(d))

    def w_first():
        rcopy(wb.at[x, k, y], wb.at[x, k, y], sw.at[0], rwa, wdest).wait_recv()
        for d in (1, 3, 2):
            wz(d).start()

    def w_second():
        for d in (1, 3, 2):
            wz_wait(d)
        for d in (1, 3, 2):
            wa2(d, y).start()
            wb2(d, x).start()

    def w_third_y():
        for d in (1, 3, 2):
            wb2(d, (x + 4 - d) % 4).wait_recv()
        for d in (1, 3, 2):
            wb3(d, y).start()

    def w_third_x():
        for d in (1, 3, 2):
            wa2(d, (y + 4 - d) % 4).wait_recv()
        for d in (1, 3, 2):
            wa3(d, x).start()

    def w_last():
        for d in (1, 3, 2):
            wa3(d, (x + 4 - d) % 4).wait_recv()
            wb3(d, (y + 4 - d) % 4).wait_recv()

    def o_copy(j, d):
        return rcopy(osend.at[j, d], opart.at[j, d], so.at[j, d], ro.at[j, d], row_axis(j)[1](4 - d))

    def l_copy(j, d):
        return rcopy(lsend.at[j, d], lpart.at[j, d], sl.at[j, d], rl.at[j, d], row_axis(j)[1](4 - d))

    def compute(j):
        for d in range(4):
            s_wait(j, d)
        x_wait(j, 4 - near)
        x_wait(j, 2)

        def tile(d):
            qq = qb[j, (row_axis(j)[0] + 4 - d) % 4].reshape(256, HD)
            scores = dot_t(qq, kv[0, j].reshape(2048, HD))
            top = jnp.max(scores, axis=1, keepdims=True)
            weights = jnp.exp2((scores - top) * SCALE)
            total = jnp.sum(weights, axis=1, keepdims=True)
            mixed = jnp.dot(weights.astype(BF16), kv[1, j].reshape(2048, HD), preferred_element_type=F32)
            osend[j, d] = (mixed * (1.0 / total)).astype(BF16)
            level = top * SCALE + jnp.log2(total)
            lsend[j, d] = jnp.concatenate(
                [jnp.broadcast_to(to_row(level[:128]), (4, 128)), jnp.broadcast_to(to_row(level[128:]), (4, 128))],
                axis=0,
            )

        def pair(u, carry):
            d0, d1 = 2 * u + 1, (2 * u + 2) % 4
            tile(d0)
            tile(d1)
            o_copy(j, d0).start()
            l_copy(j, d0).start()

            @pl.when(u == 0)
            def _():
                o_copy(j, d1).start()
                l_copy(j, d1).start()

            return carry

        lax.fori_loop(0, 2, pair, 0)

    oq = k % 2
    ob = k // 2

    def r_copy(j, h):
        return rcopy(ored.at[j, h], oz.at[ob, j], sr.at[j, h], rz.at[ob, j], dev(oq, x, 2 * c + h, y, r))

    def r_same(h):
        return jnp.logical_and(2 * c + h == k, oq == c)

    def merge(j):
        for d in range(1, 4):
            o_copy(j, d).wait_recv()
            l_copy(j, d).wait_recv()
        levels = [lsend[j, 0]] + [lpart[j, d] for d in range(1, 4)]
        best = jnp.maximum(jnp.maximum(levels[0], levels[1]), jnp.maximum(levels[2], levels[3]))
        parts = [jnp.exp2(v - best) for v in levels]
        inv = 1.0 / (parts[0] + parts[1] + parts[2] + parts[3])
        for h in range(2):
            total = None
            for d in range(4):
                share_d = to_col((parts[d] * inv)[4 * h:4 * h + 1])
                rows = pl.ds(128 * h, 128)
                block = osend[j, 0, rows, :] if d == 0 else opart[j, d, rows, :]
                term = block.astype(F32) * share_d
                total = term if total is None else total + term
            ored[j, h] = total.astype(BF16)
        for h in range(2):
            @pl.when(r_same(h))
            def _():
                pltpu.make_async_copy(ored.at[j, h], oz.at[ob, j], rz.at[ob, j]).start()

            @pl.when(jnp.logical_not(r_same(h)))
            def _():
                r_copy(j, h).start()

    sigma = to_col(0.5 * jnp.exp(math.log(8.0) * step_in[...].astype(F32) / (NSTEPS - 1)))
    factor = 1.0 + (guide_scale - 1.0) * to_col(mask_in[...].astype(F32))

    def c_lanes(rr, qq, j):
        return pl.ds(pl.multiple_of(128 * (6 * rr + 3 * qq + j), 128), 128)

    def c_peer(n):
        return (c if n == 1 else 1 - c), (r if n == 0 else 1 - r)

    def c_copy(j, n):
        cc, rr = c_peer(n)
        lanes = c_lanes(r, c, j)
        return rcopy(cmb.at[:, lanes], cmb.at[:, lanes], sc.at[j, n], rc.at[j, n], dev(cc, x, k, y, rr))

    def c_wait(j, n):
        cc, rr = c_peer(n)
        lanes = c_lanes(rr, cc, j)
        rcopy(cmb.at[:, lanes], cmb.at[:, lanes], sc.at[j, n], rc.at[j, n], dev(cc, x, k, y, rr)).wait_recv()

    def combine(j):
        for b in range(2):
            rcopy(oz.at[b, j], oz.at[b, j], sr.at[j, 0], rz.at[b, j], dev(1 - c, x, k, y, r)).wait_recv()
        guided = factor * oz[0, j].astype(F32) + (1.0 - factor) * oz[1, j].astype(F32)
        cmb[:, c_lanes(r, c, j)] = guided.astype(BF16)
        for n in (1, 2, 0):
            c_copy(j, n).start()

    relay(0)
    w_first()
    relay(1)
    forward(0)
    share(0)
    relay(2)
    forward(1)
    compute(0)
    share(1)
    forward(2)
    w_second()
    compute(1)
    share(2)
    w_third_y()
    merge(0)
    compute(2)
    w_third_x()
    merge(1)
    combine(0)
    merge(2)
    combine(1)
    combine(2)
    for j in range(3):
        for n in range(3):
            c_wait(j, n)
    w_last()
    guided = dot_t(cmb[:, 0:384], wb[0].reshape(768, 384))
    for n in range(1, 4):
        guided += dot_t(cmb[:, 384 * n:384 * n + 384], wb[n].reshape(768, 384))
    out_ref[...] = (lat[...].astype(F32) - sigma * guided).astype(BF16)

    for j in range(3):
        for q in range(2):
            for t in range(3):
                copy, _src, _dst, _sem, same = z_remote(j, q, t)

                @pl.when(jnp.logical_not(same))
                def _():
                    copy.wait_send()

        for d in range(1, 4):
            x_copy(j, d, 0, 1).wait_send()
            y_copy(j, d, 0, 1).wait_send()
            o_copy(j, d).wait_send()
            l_copy(j, d).wait_send()
        for d in range(4):
            s_copy(j, d).wait_send()
        for h in range(2):
            @pl.when(jnp.logical_not(r_same(h)))
            def _():
                r_copy(j, h).wait_send()

        for n in range(3):
            c_copy(j, n).wait_send()

    @pl.when(jnp.logical_not(wself))
    def _():
        wcopy.wait_send()

    for d in range(1, 4):
        wz(d).wait_send()
        wa2(d, y).wait_send()
        wb2(d, x).wait_send()
        wa3(d, x).wait_send()
        wb3(d, y).wait_send()


def on_device(queries, keyvals, out_weight, latent, timestep, cond_mask):
    rows = queries.shape[1]
    dma = pltpu.SemaphoreType.DMA
    vmem = pltpu.VMEM
    anywhere = pl.BlockSpec(memory_space=pl.ANY)
    return pl.pallas_call(
        kernel,
        out_shape=jax.ShapeDtypeStruct((rows, 768), BF16),
        in_specs=[anywhere] * 4 + [pl.BlockSpec(memory_space=vmem)] * 2,
        out_specs=pl.BlockSpec(memory_space=vmem),
        scratch_shapes=[
            vmem((rows, 768), BF16),
            vmem((2, rows, 768), BF16),
            vmem((48, 768), BF16),
            vmem((rows, 768), BF16),
            vmem((2, 3, 4, 4, 128, HD), BF16),
            vmem((3, 4, 2, 128, HD), BF16),
            vmem((3, 4, 256, HD), BF16),
            vmem((3, 4, 256, HD), BF16),
            vmem((3, 4, 8, 128), F32),
            vmem((3, 4, 8, 128), F32),
            vmem((3, 2, 128, HD), BF16),
            vmem((2, 3, 128, HD), BF16),
            vmem((128, 1536), BF16),
            vmem((4, 4, 4, 48, 384), BF16),
            dma((3, 2, 3)), dma((3, 4)), dma((3, 4)), dma((3, 4)), dma((3, 4)), dma((3, 4)),
            dma((3, 2)), dma((3, 3)), dma((16,)),
            dma((3,)), dma((3,)), dma((3, 4)), dma((3, 4)), dma((3, 4)), dma((3, 4)), dma((3, 4)),
            dma((2, 3)), dma((3, 3)), dma, dma((5, 4)), dma((4,)),
        ],
        compiler_params=pltpu.CompilerParams(
            collective_id=0, has_side_effects=True, vmem_limit_bytes=58 << 20
        ),
    )(queries[0], keyvals[0], out_weight.T, latent, timestep.reshape(1, rows), cond_mask.reshape(1, rows))


def solution(mesh):
    placed = (
        P("cfg", "seq", "rep"),
        P("cfg", None, "seq", "rep"),
        P("rep", "seq"),
        P("seq", ("cfg", "rep")),
        P("seq"),
        P("seq"),
    )
    return jax.shard_map(
        on_device, mesh=mesh, in_specs=placed, out_specs=P("seq", ("cfg", "rep")), check_vma=False
    )
```

```python
import math

import jax
import jax.numpy as jnp
from jax import lax
from jax.experimental import pallas as pl
from jax.experimental.pallas import tpu as pltpu
from jax.sharding import PartitionSpec as P

HD = 128
NSTEPS = 50
guide_scale = 3.0
SCALE = math.log2(math.e) / math.sqrt(HD)
MESH = pl.DeviceIdType.MESH
F32 = jnp.float32
BF16 = jnp.bfloat16


def dot_t(a, b):
    return lax.dot_general(a, b, (((1,), (1,)), ((), ())), preferred_element_type=F32)


def rcopy(src, dst, send_sem, recv_sem, device):
    return pltpu.make_async_remote_copy(
        src_ref=src, dst_ref=dst, send_sem=send_sem, recv_sem=recv_sem,
        device_id=device, device_id_type=MESH,
    )


def kernel(q_hbm, kv_hbm, w_hbm, latent_hbm, step_in, mask_in, out_ref,
           q_in, kv_in, wt, lat, kv, qb, osend, opart, lsend, lpart, ored, oz, cmb, wb,
           sz, sy, ss, sx, so, sl, sr, sc, sw,
           rt, rq, ry, rs, rx, ro, rl, rz, rc, rwa, rw, sin):
    c = lax.axis_index("cfg")
    s = lax.axis_index("seq")
    r = lax.axis_index("rep")
    x, k, y = s // 16, (s // 4) % 4, s % 4

    def dev(c_, x_, k_, y_, r_):
        return (c_, x_ * 16 + k_ * 4 + y_, r_)

    def xdev(d):
        return dev(c, (x + d) % 4, k, y, r)

    def ydev(d):
        return dev(c, x, k, (y + d) % 4, r)

    def zdev(d):
        return dev(c, x, (k + d) % 4, y, r)

    wdx, wsx = 2 * r + c, 2 * c + r
    wdest = dev(x // 2, wdx, k, y, x % 2)
    wsrc = dev(x % 2, wsx, k, y, x // 2)
    wself = jnp.logical_and(jnp.logical_and(wdx == x, x // 2 == c), x % 2 == r)

    barrier = pltpu.get_barrier_semaphore()

    def hello(device):
        pl.semaphore_signal(barrier, inc=1, device_id=device, device_id_type=MESH)

    for d in range(1, 4):
        hello(xdev(d))
        hello(ydev(d))
        hello(zdev(d))
    for d in range(4):
        hello(dev(1 - c, x, (k + d) % 4, y, r))
    hello(dev(c, x, k, y, 1 - r))
    hello(dev(1 - c, x, k, y, 1 - r))

    @pl.when(jnp.logical_not(wself))
    def _():
        hello(wdest)
        hello(wsrc)

    staged = [
        pltpu.make_async_copy(src, dst, sin.at[n])
        for n, (src, dst) in enumerate(((q_hbm, q_in), (kv_hbm, kv_in), (w_hbm, wt), (latent_hbm, lat)))
    ]
    for copy in staged:
        copy.start()
    eye = lax.broadcasted_iota(jnp.int32, (128, 128), 0) == lax.broadcasted_iota(jnp.int32, (128, 128), 1)

    def to_row(col):
        return jnp.sum(jnp.where(eye, jnp.broadcast_to(col, (128, 128)), 0.0), axis=0, keepdims=True)

    def to_col(row):
        return jnp.sum(jnp.where(eye, jnp.broadcast_to(row, (128, 128)), 0.0), axis=1, keepdims=True)

    for copy in staged:
        copy.wait()
    pl.semaphore_wait(barrier, jnp.where(wself, 15, 17))

    def row_axis(j):
        return (y, ydev) if j == 1 else (x, xdev)

    def key_axis(j):
        return (x, xdev) if j == 1 else (y, ydev)

    def z_copies(j, q, t):
        kd = 2 * c + q
        lanes = pl.ds(384 * q + 128 * j, 128)
        if t == 2:
            core = k // 2
            return (q_in.at[:, lanes], qb.at[j, row_axis(j)[0], k % 2], rq.at[j], core, kd, kd == k)
        return (kv_in.at[t, :, lanes], kv.at[t, j, key_axis(j)[0], k], rt.at[j], t, kd, jnp.logical_and(kd == k, c == t))

    def z_remote(j, q, t):
        src, dst, sem, core, kd, same = z_copies(j, q, t)
        return rcopy(src, dst, sz.at[j, q, t], sem, dev(core, x, kd, y, r)), src, dst, sem, same

    for j in range(3):
        for t in (2, 0, 1):
            for q in range(2):
                copy, src, dst, sem, same = z_remote(j, q, t)

                @pl.when(same)
                def _():
                    pltpu.make_async_copy(src, dst, sem).start()

                @pl.when(jnp.logical_not(same))
                def _():
                    copy.start()

    wcopy = rcopy(wt.at[:, pl.ds(pl.multiple_of(384 * c, 128), 384)],
                  wb.at[wdx, k, y], sw.at[0], rwa, wdest)

    @pl.when(wself)
    def _():
        pltpu.make_async_copy(wt.at[:, pl.ds(pl.multiple_of(384 * c, 128), 384)],
                              wb.at[x, k, y], rwa).start()

    @pl.when(jnp.logical_not(wself))
    def _():
        wcopy.start()

    near = 1 + 2 * c

    def x_copy(j, d, src, to):
        block = qb.at[j, src]
        return rcopy(block, block, sx.at[j, d], rx.at[j, d], row_axis(j)[1](to))

    def x_send(j, d):
        return x_copy(j, d, row_axis(j)[0], d)

    def x_pass(j):
        return x_copy(j, 2, (row_axis(j)[0] + 4 - near) % 4, near)

    def x_wait(j, d):
        x_copy(j, d, (row_axis(j)[0] + 4 - d) % 4, d).wait_recv()

    def y_copy(j, d, src, to):
        block = kv.at[c, j, src]
        return rcopy(block, block, sy.at[j, d], ry.at[j, d], key_axis(j)[1](to))

    def y_send(j, d):
        return y_copy(j, d, key_axis(j)[0], d)

    def y_pass(j):
        return y_copy(j, 2, (key_axis(j)[0] + 4 - near) % 4, near)

    def y_wait(j, d):
        y_copy(j, d, (key_axis(j)[0] + 4 - d) % 4, d).wait_recv()

    def s_copy(j, d):
        block = kv.at[c, j, (key_axis(j)[0] + 4 - d) % 4]
        return rcopy(block, block, ss.at[j, d], rs.at[j, d], dev(1 - c, x, k, y, r))

    def s_wait(j, d):
        block = kv.at[1 - c, j, (key_axis(j)[0] + 4 - d) % 4]
        rcopy(block, block, ss.at[j, d], rs.at[j, d], dev(1 - c, x, k, y, r)).wait_recv()

    def relay(j):
        own = qb.at[j, row_axis(j)[0]]
        rcopy(own, own, sx.at[j, 0], rq.at[j], xdev(1)).wait_recv()
        for d in (1, 3):
            x_send(j, d).start()
        own = kv.at[c, j, key_axis(j)[0]]
        rcopy(own, own, sx.at[j, 0], rt.at[j], ydev(1)).wait_recv()
        for d in (1, 3):
            y_send(j, d).start()
        s_copy(j, 0).start()

    def forward(j):
        x_wait(j, near)
        x_pass(j).start()
        y_wait(j, near)
        y_pass(j).start()
        s_copy(j, near).start()
        y_wait(j, 4 - near)
        s_copy(j, 4 - near).start()

    def share(j):
        y_wait(j, 2)
        s_copy(j, 2).start()

    lo, hi = pl.ds(0, 2), pl.ds(2, 2)

    def wz(d):
        return rcopy(wb.at[x, k, y], wb.at[x, k, y], sw.at[d], rw.at[0, d], zdev(d))

    def wz_wait(d):
        kk = (k + 4 - d) % 4
        rcopy(wb.at[x, kk, y], wb.at[x, kk, y], sw.at[d], rw.at[0, d], zdev(d)).wait_recv()

    def wa2(d, yy):
        return rcopy(wb.at[x, lo, yy], wb.at[x, lo, yy], sw.at[3 + d], rw.at[1, d], ydev(d))

    def wb2(d, xx):
        return rcopy(wb.at[xx, hi, y], wb.at[xx, hi, y], sw.at[6 + d], rw.at[2, d], xdev(d))

    def wa3(d, xx, n):
        block = wb.at[xx, n]
        return rcopy(block, block, sw.at[16 + 4 * n + d], rw.at[3 + n, d], xdev(d))

    def wb3(d, yy, n):
        block = wb.at[:, 2 + n, yy]
        return rcopy(block, block, sw.at[24 + 4 * n + d], rw.at[5 + n, d], ydev(d))

    def w_first():
        rcopy(wb.at[x, k, y], wb.at[x, k, y], sw.at[0], rwa, wdest).wait_recv()
        for d in (1, 3, 2):
            wz(d).start()

    def w_second():
        for d in (1, 3, 2):
            wz_wait(d)
        for d in (1, 3, 2):
            wa2(d, y).start()
            wb2(d, x).start()

    def w_wait_b2():
        for d in (1, 3, 2):
            wb2(d, (x + 4 - d) % 4).wait_recv()

    def w_wait_a2():
        for d in (1, 3, 2):
            wa2(d, (y + 4 - d) % 4).wait_recv()

    def w_y(n):
        for d in (1, 3, 2):
            wb3(d, y, n).start()

    def w_x(n):
        for d in (1, 3, 2):
            wa3(d, x, n).start()

    def w_last():
        for d in (1, 3, 2):
            for n in range(2):
                wa3(d, (x + 4 - d) % 4, n).wait_recv()
                wb3(d, (y + 4 - d) % 4, n).wait_recv()

    def o_copy(j, d):
        return rcopy(osend.at[j, d], opart.at[j, d], so.at[j, d], ro.at[j, d], row_axis(j)[1](4 - d))

    def l_copy(j, d):
        return rcopy(lsend.at[j, d], lpart.at[j, d], sl.at[j, d], rl.at[j, d], row_axis(j)[1](4 - d))

    def compute(j):
        for d in range(4):
            s_wait(j, d)
        x_wait(j, 4 - near)
        x_wait(j, 2)

        def tile(d):
            qq = qb[j, (row_axis(j)[0] + 4 - d) % 4].reshape(256, HD)
            scores = dot_t(qq, kv[0, j].reshape(2048, HD))
            top = jnp.max(scores, axis=1, keepdims=True)
            weights = jnp.exp2((scores - top) * SCALE)
            total = jnp.sum(weights, axis=1, keepdims=True)
            mixed = jnp.dot(weights.astype(BF16), kv[1, j].reshape(2048, HD), preferred_element_type=F32)
            osend[j, d] = (mixed * (1.0 / total)).astype(BF16)
            level = top * SCALE + jnp.log2(total)
            lsend[j, d] = jnp.concatenate(
                [jnp.broadcast_to(to_row(level[:128]), (4, 128)), jnp.broadcast_to(to_row(level[128:]), (4, 128))],
                axis=0,
            )

        def pair(u, carry):
            d0, d1 = 2 * u + 1, (2 * u + 2) % 4
            tile(d0)
            tile(d1)
            o_copy(j, d0).start()
            l_copy(j, d0).start()

            @pl.when(u == 0)
            def _():
                o_copy(j, d1).start()
                l_copy(j, d1).start()

            return carry

        lax.fori_loop(0, 2, pair, 0)

    oq = k % 2
    ob = k // 2

    def r_copy(j, h):
        return rcopy(ored.at[j, h], oz.at[ob, j], sr.at[j, h], rz.at[ob, j], dev(oq, x, 2 * c + h, y, r))

    def r_same(h):
        return jnp.logical_and(2 * c + h == k, oq == c)

    def merge(j):
        for d in range(1, 4):
            o_copy(j, d).wait_recv()
            l_copy(j, d).wait_recv()
        levels = [lsend[j, 0]] + [lpart[j, d] for d in range(1, 4)]
        best = jnp.maximum(jnp.maximum(levels[0], levels[1]), jnp.maximum(levels[2], levels[3]))
        parts = [jnp.exp2(v - best) for v in levels]
        inv = 1.0 / (parts[0] + parts[1] + parts[2] + parts[3])
        for h in range(2):
            total = None
            for d in range(4):
                share_d = to_col((parts[d] * inv)[4 * h:4 * h + 1])
                rows = pl.ds(128 * h, 128)
                block = osend[j, 0, rows, :] if d == 0 else opart[j, d, rows, :]
                term = block.astype(F32) * share_d
                total = term if total is None else total + term
            ored[j, h] = total.astype(BF16)
        for h in range(2):
            @pl.when(r_same(h))
            def _():
                pltpu.make_async_copy(ored.at[j, h], oz.at[ob, j], rz.at[ob, j]).start()

            @pl.when(jnp.logical_not(r_same(h)))
            def _():
                r_copy(j, h).start()

    sigma = to_col(0.5 * jnp.exp(math.log(8.0) * step_in[...].astype(F32) / (NSTEPS - 1)))
    factor = 1.0 + (guide_scale - 1.0) * to_col(mask_in[...].astype(F32))

    def c_lanes(rr, qq, j):
        return pl.ds(pl.multiple_of(128 * (6 * rr + 3 * qq + j), 128), 128)

    def c_peer(n):
        return (c if n == 1 else 1 - c), (r if n == 0 else 1 - r)

    def c_copy(j, n):
        cc, rr = c_peer(n)
        lanes = c_lanes(r, c, j)
        return rcopy(cmb.at[:, lanes], cmb.at[:, lanes], sc.at[j, n], rc.at[j, n], dev(cc, x, k, y, rr))

    def c_wait(j, n):
        cc, rr = c_peer(n)
        lanes = c_lanes(rr, cc, j)
        rcopy(cmb.at[:, lanes], cmb.at[:, lanes], sc.at[j, n], rc.at[j, n], dev(cc, x, k, y, rr)).wait_recv()

    def combine(j):
        for b in range(2):
            rcopy(oz.at[b, j], oz.at[b, j], sr.at[j, 0], rz.at[b, j], dev(1 - c, x, k, y, r)).wait_recv()
        guided = factor * oz[0, j].astype(F32) + (1.0 - factor) * oz[1, j].astype(F32)
        cmb[:, c_lanes(r, c, j)] = guided.astype(BF16)
        for n in (1, 2, 0):
            c_copy(j, n).start()

    relay(0)
    w_first()
    relay(1)
    forward(0)
    share(0)
    relay(2)
    forward(1)
    compute(0)
    share(1)
    forward(2)
    w_second()
    compute(1)
    share(2)
    merge(0)
    compute(2)
    w_wait_b2()
    w_wait_a2()
    w_x(0)
    w_y(0)
    w_x(1)
    w_y(1)
    merge(1)
    combine(0)
    merge(2)
    combine(1)
    combine(2)
    for j in range(3):
        for n in range(3):
            c_wait(j, n)
    w_last()
    guided = dot_t(cmb[:, 0:384], wb[0].reshape(768, 384))
    for n in range(1, 4):
        guided += dot_t(cmb[:, 384 * n:384 * n + 384], wb[n].reshape(768, 384))
    out_ref[...] = (lat[...].astype(F32) - sigma * guided).astype(BF16)

    for j in range(3):
        for q in range(2):
            for t in range(3):
                copy, _src, _dst, _sem, same = z_remote(j, q, t)

                @pl.when(jnp.logical_not(same))
                def _():
                    copy.wait_send()

        for d in range(1, 4):
            x_copy(j, d, 0, 1).wait_send()
            y_copy(j, d, 0, 1).wait_send()
            o_copy(j, d).wait_send()
            l_copy(j, d).wait_send()
        for d in range(4):
            s_copy(j, d).wait_send()
        for h in range(2):
            @pl.when(jnp.logical_not(r_same(h)))
            def _():
                r_copy(j, h).wait_send()

        for n in range(3):
            c_copy(j, n).wait_send()

    @pl.when(jnp.logical_not(wself))
    def _():
        wcopy.wait_send()

    for d in range(1, 4):
        wz(d).wait_send()
        wa2(d, y).wait_send()
        wb2(d, x).wait_send()
        for n in range(2):
            wa3(d, x, n).wait_send()
            wb3(d, y, n).wait_send()


def on_device(queries, keyvals, out_weight, latent, timestep, cond_mask):
    rows = queries.shape[1]
    dma = pltpu.SemaphoreType.DMA
    vmem = pltpu.VMEM
    anywhere = pl.BlockSpec(memory_space=pl.ANY)
    return pl.pallas_call(
        kernel,
        out_shape=jax.ShapeDtypeStruct((rows, 768), BF16),
        in_specs=[anywhere] * 4 + [pl.BlockSpec(memory_space=vmem)] * 2,
        out_specs=pl.BlockSpec(memory_space=vmem),
        scratch_shapes=[
            vmem((rows, 768), BF16),
            vmem((2, rows, 768), BF16),
            vmem((48, 768), BF16),
            vmem((rows, 768), BF16),
            vmem((2, 3, 4, 4, 128, HD), BF16),
            vmem((3, 4, 2, 128, HD), BF16),
            vmem((3, 4, 256, HD), BF16),
            vmem((3, 4, 256, HD), BF16),
            vmem((3, 4, 8, 128), F32),
            vmem((3, 4, 8, 128), F32),
            vmem((3, 2, 128, HD), BF16),
            vmem((2, 3, 128, HD), BF16),
            vmem((128, 1536), BF16),
            vmem((4, 4, 4, 48, 384), BF16),
            dma((3, 2, 3)), dma((3, 4)), dma((3, 4)), dma((3, 4)), dma((3, 4)), dma((3, 4)),
            dma((3, 2)), dma((3, 3)), dma((32,)),
            dma((3,)), dma((3,)), dma((3, 4)), dma((3, 4)), dma((3, 4)), dma((3, 4)), dma((3, 4)),
            dma((2, 3)), dma((3, 3)), dma, dma((7, 4)), dma((4,)),
        ],
        compiler_params=pltpu.CompilerParams(
            collective_id=0, has_side_effects=True, vmem_limit_bytes=58 << 20
        ),
    )(queries[0], keyvals[0], out_weight.T, latent, timestep.reshape(1, rows), cond_mask.reshape(1, rows))


def solution(mesh):
    placed = (
        P("cfg", "seq", "rep"),
        P("cfg", None, "seq", "rep"),
        P("rep", "seq"),
        P("seq", ("cfg", "rep")),
        P("seq"),
        P("seq"),
    )
    return jax.shard_map(
        on_device, mesh=mesh, in_specs=placed, out_specs=P("seq", ("cfg", "rep")), check_vma=False
    )
```

```python
import math

import jax
import jax.numpy as jnp
from jax import lax
from jax.experimental import pallas as pl
from jax.experimental.pallas import tpu as pltpu
from jax.sharding import PartitionSpec as P

HD = 128
NSTEPS = 50
guide_scale = 3.0
SCALE = math.log2(math.e) / math.sqrt(HD)
MESH = pl.DeviceIdType.MESH
F32 = jnp.float32
BF16 = jnp.bfloat16


def dot_t(a, b):
    return lax.dot_general(a, b, (((1,), (1,)), ((), ())), preferred_element_type=F32)


def rcopy(src, dst, send_sem, recv_sem, device):
    return pltpu.make_async_remote_copy(
        src_ref=src, dst_ref=dst, send_sem=send_sem, recv_sem=recv_sem,
        device_id=device, device_id_type=MESH,
    )


def kernel(q_hbm, kv_hbm, w_hbm, latent_hbm, step_in, mask_in, out_ref,
           q_in, kv_in, wt, lat, kv, qb, osend, opart, lsend, lpart, ored, oz, cmb, wb,
           sz, sy, ss, sx, so, sl, sr, sc, sw,
           rt, rq, ry, rs, rx, ro, rl, rz, rc, rwa, rw, sin):
    c = lax.axis_index("cfg")
    s = lax.axis_index("seq")
    r = lax.axis_index("rep")
    x, k, y = s // 16, (s // 4) % 4, s % 4

    def dev(c_, x_, k_, y_, r_):
        return (c_, x_ * 16 + k_ * 4 + y_, r_)

    def xdev(d):
        return dev(c, (x + d) % 4, k, y, r)

    def ydev(d):
        return dev(c, x, k, (y + d) % 4, r)

    def zdev(d):
        return dev(c, x, (k + d) % 4, y, r)

    wdx, wsx = 2 * r + c, 2 * c + r
    wdest = dev(x // 2, wdx, k, y, x % 2)
    wsrc = dev(x % 2, wsx, k, y, x // 2)
    wself = jnp.logical_and(jnp.logical_and(wdx == x, x // 2 == c), x % 2 == r)

    barrier = pltpu.get_barrier_semaphore()

    def hello(device):
        pl.semaphore_signal(barrier, inc=1, device_id=device, device_id_type=MESH)

    for d in range(1, 4):
        hello(xdev(d))
        hello(ydev(d))
        hello(zdev(d))
    for d in range(4):
        hello(dev(1 - c, x, (k + d) % 4, y, r))
    hello(dev(c, x, k, y, 1 - r))
    hello(dev(1 - c, x, k, y, 1 - r))

    @pl.when(jnp.logical_not(wself))
    def _():
        hello(wdest)
        hello(wsrc)

    staged = [
        pltpu.make_async_copy(src, dst, sin.at[n])
        for n, (src, dst) in enumerate(((q_hbm, q_in), (kv_hbm, kv_in), (w_hbm, wt), (latent_hbm, lat)))
    ]
    for copy in staged:
        copy.start()
    eye = lax.broadcasted_iota(jnp.int32, (128, 128), 0) == lax.broadcasted_iota(jnp.int32, (128, 128), 1)

    def to_row(col):
        return jnp.sum(jnp.where(eye, jnp.broadcast_to(col, (128, 128)), 0.0), axis=0, keepdims=True)

    def to_col(row):
        return jnp.sum(jnp.where(eye, jnp.broadcast_to(row, (128, 128)), 0.0), axis=1, keepdims=True)

    for copy in staged:
        copy.wait()
    pl.semaphore_wait(barrier, jnp.where(wself, 15, 17))

    def row_axis(j):
        return (y, ydev) if j == 1 else (x, xdev)

    def key_axis(j):
        return (x, xdev) if j == 1 else (y, ydev)

    def z_copies(j, q, t):
        kd = 2 * c + q
        lanes = pl.ds(384 * q + 128 * j, 128)
        if t == 2:
            core = k // 2
            return (q_in.at[:, lanes], qb.at[j, row_axis(j)[0], k % 2], rq.at[j], core, kd, kd == k)
        return (kv_in.at[t, :, lanes], kv.at[t, j, key_axis(j)[0], k], rt.at[j], t, kd, jnp.logical_and(kd == k, c == t))

    def z_remote(j, q, t):
        src, dst, sem, core, kd, same = z_copies(j, q, t)
        return rcopy(src, dst, sz.at[j, q, t], sem, dev(core, x, kd, y, r)), src, dst, sem, same

    for j in range(3):
        for t in (2, 0, 1):
            for q in range(2):
                copy, src, dst, sem, same = z_remote(j, q, t)

                @pl.when(same)
                def _():
                    pltpu.make_async_copy(src, dst, sem).start()

                @pl.when(jnp.logical_not(same))
                def _():
                    copy.start()

    wcopy = rcopy(wt.at[:, pl.ds(pl.multiple_of(384 * c, 128), 384)],
                  wb.at[wdx, k, y], sw.at[0], rwa, wdest)

    @pl.when(wself)
    def _():
        pltpu.make_async_copy(wt.at[:, pl.ds(pl.multiple_of(384 * c, 128), 384)],
                              wb.at[x, k, y], rwa).start()

    @pl.when(jnp.logical_not(wself))
    def _():
        wcopy.start()

    near = 1 + 2 * c

    def x_copy(j, d, src, to):
        block = qb.at[j, src]
        return rcopy(block, block, sx.at[j, d], rx.at[j, d], row_axis(j)[1](to))

    def x_send(j, d):
        return x_copy(j, d, row_axis(j)[0], d)

    def x_pass(j):
        return x_copy(j, 2, (row_axis(j)[0] + 4 - near) % 4, near)

    def x_wait(j, d):
        x_copy(j, d, (row_axis(j)[0] + 4 - d) % 4, d).wait_recv()

    def y_copy(j, d, src, to):
        block = kv.at[c, j, src]
        return rcopy(block, block, sy.at[j, d], ry.at[j, d], key_axis(j)[1](to))

    def y_send(j, d):
        return y_copy(j, d, key_axis(j)[0], d)

    def y_pass(j):
        return y_copy(j, 2, (key_axis(j)[0] + 4 - near) % 4, near)

    def y_wait(j, d):
        y_copy(j, d, (key_axis(j)[0] + 4 - d) % 4, d).wait_recv()

    def s_copy(j, d):
        block = kv.at[c, j, (key_axis(j)[0] + 4 - d) % 4]
        return rcopy(block, block, ss.at[j, d], rs.at[j, d], dev(1 - c, x, k, y, r))

    def s_wait(j, d):
        block = kv.at[1 - c, j, (key_axis(j)[0] + 4 - d) % 4]
        rcopy(block, block, ss.at[j, d], rs.at[j, d], dev(1 - c, x, k, y, r)).wait_recv()

    def relay(j):
        own = qb.at[j, row_axis(j)[0]]
        rcopy(own, own, sx.at[j, 0], rq.at[j], xdev(1)).wait_recv()
        for d in (1, 3):
            x_send(j, d).start()
        own = kv.at[c, j, key_axis(j)[0]]
        rcopy(own, own, sx.at[j, 0], rt.at[j], ydev(1)).wait_recv()
        for d in (1, 3):
            y_send(j, d).start()
        s_copy(j, 0).start()

    def forward(j):
        x_wait(j, near)
        x_pass(j).start()
        y_wait(j, near)
        y_pass(j).start()
        s_copy(j, near).start()
        y_wait(j, 4 - near)
        s_copy(j, 4 - near).start()

    def share(j):
        y_wait(j, 2)
        s_copy(j, 2).start()

    lo, hi = pl.ds(0, 2), pl.ds(2, 2)
    main, rest = pl.ds(0, 40), pl.ds(40, 8)

    def wz(d, kk):
        block = wb.at[x, kk, y, main]
        return rcopy(block, block, sw.at[d], rw.at[0, d], zdev(d))

    def wa2(d, yy):
        block = wb.at[x, lo, yy, main]
        return rcopy(block, block, sw.at[3 + d], rw.at[1, d], ydev(d))

    def wb2(d, xx):
        block = wb.at[xx, hi, y, main]
        return rcopy(block, block, sw.at[6 + d], rw.at[2, d], xdev(d))

    def wa3(d, xx, n):
        block = wb.at[xx, n, :, main]
        return rcopy(block, block, sw.at[16 + 4 * n + d], rw.at[3 + n, d], xdev(d))

    def wb3(d, yy, n):
        block = wb.at[:, 2 + n, yy, main]
        return rcopy(block, block, sw.at[24 + 4 * n + d], rw.at[5 + n, d], ydev(d))

    def wc1(d, xx):
        block = wb.at[xx, k, y, rest]
        return rcopy(block, block, sw.at[32 + d], rw.at[7, d], xdev(d))

    def wc2(d, yy):
        block = wb.at[:, k, yy, rest]
        return rcopy(block, block, sw.at[36 + d], rw.at[8, d], ydev(d))

    def wc3(d, kk):
        block = wb.at[:, kk, :, rest]
        return rcopy(block, block, sw.at[40 + d], rw.at[9, d], zdev(d))

    def w_rest():
        for d in (1, 3, 2):
            wc1(d, (x + 4 - d) % 4).wait_recv()
        for d in (1, 3, 2):
            wc2(d, y).start()

    def w_rest_z():
        for d in (1, 3, 2):
            wc2(d, (y + 4 - d) % 4).wait_recv()
        for d in (1, 3, 2):
            wc3(d, k).start()

    def w_first():
        rcopy(wb.at[x, k, y], wb.at[x, k, y], sw.at[0], rwa, wdest).wait_recv()
        for d in (1, 3, 2):
            wc1(d, x).start()
        for d in (1, 3, 2):
            wz(d, k).start()

    def w_second():
        for d in (1, 3, 2):
            wz(d, (k + 4 - d) % 4).wait_recv()
        for d in (1, 3, 2):
            wa2(d, y).start()
            wb2(d, x).start()

    def w_wait_b2():
        for d in (1, 3, 2):
            wb2(d, (x + 4 - d) % 4).wait_recv()

    def w_wait_a2():
        for d in (1, 3, 2):
            wa2(d, (y + 4 - d) % 4).wait_recv()

    def w_y(n):
        for d in (1, 3, 2):
            wb3(d, y, n).start()

    def w_x(n):
        for d in (1, 3, 2):
            wa3(d, x, n).start()

    def w_last():
        for d in (1, 3, 2):
            wc3(d, (k + 4 - d) % 4).wait_recv()
        for d in (1, 3, 2):
            for n in range(2):
                wa3(d, (x + 4 - d) % 4, n).wait_recv()
                wb3(d, (y + 4 - d) % 4, n).wait_recv()

    def o_copy(j, d):
        return rcopy(osend.at[j, d], opart.at[j, d], so.at[j, d], ro.at[j, d], row_axis(j)[1](4 - d))

    def l_copy(j, d):
        return rcopy(lsend.at[j, d], lpart.at[j, d], sl.at[j, d], rl.at[j, d], row_axis(j)[1](4 - d))

    def compute(j):
        for d in range(4):
            s_wait(j, d)
        x_wait(j, 4 - near)
        x_wait(j, 2)

        def tile(d):
            qq = qb[j, (row_axis(j)[0] + 4 - d) % 4].reshape(256, HD)
            scores = dot_t(qq, kv[0, j].reshape(2048, HD))
            top = jnp.max(scores, axis=1, keepdims=True)
            weights = jnp.exp2((scores - top) * SCALE)
            total = jnp.sum(weights, axis=1, keepdims=True)
            mixed = jnp.dot(weights.astype(BF16), kv[1, j].reshape(2048, HD), preferred_element_type=F32)
            osend[j, d] = (mixed * (1.0 / total)).astype(BF16)
            level = top * SCALE + jnp.log2(total)
            lsend[j, d] = jnp.concatenate(
                [jnp.broadcast_to(to_row(level[:128]), (4, 128)), jnp.broadcast_to(to_row(level[128:]), (4, 128))],
                axis=0,
            )

        def pair(u, carry):
            d0, d1 = 2 * u + 1, (2 * u + 2) % 4
            tile(d0)
            tile(d1)
            o_copy(j, d0).start()
            l_copy(j, d0).start()

            @pl.when(u == 0)
            def _():
                o_copy(j, d1).start()
                l_copy(j, d1).start()

            return carry

        lax.fori_loop(0, 2, pair, 0)

    oq = k % 2
    ob = k // 2

    def r_copy(j, h):
        return rcopy(ored.at[j, h], oz.at[ob, j], sr.at[j, h], rz.at[ob, j], dev(oq, x, 2 * c + h, y, r))

    def r_same(h):
        return jnp.logical_and(2 * c + h == k, oq == c)

    def merge(j):
        for d in range(1, 4):
            o_copy(j, d).wait_recv()
            l_copy(j, d).wait_recv()
        levels = [lsend[j, 0]] + [lpart[j, d] for d in range(1, 4)]
        best = jnp.maximum(jnp.maximum(levels[0], levels[1]), jnp.maximum(levels[2], levels[3]))
        parts = [jnp.exp2(v - best) for v in levels]
        inv = 1.0 / (parts[0] + parts[1] + parts[2] + parts[3])
        for h in range(2):
            total = None
            for d in range(4):
                share_d = to_col((parts[d] * inv)[4 * h:4 * h + 1])
                rows = pl.ds(128 * h, 128)
                block = osend[j, 0, rows, :] if d == 0 else opart[j, d, rows, :]
                term = block.astype(F32) * share_d
                total = term if total is None else total + term
            ored[j, h] = total.astype(BF16)
        for h in range(2):
            @pl.when(r_same(h))
            def _():
                pltpu.make_async_copy(ored.at[j, h], oz.at[ob, j], rz.at[ob, j]).start()

            @pl.when(jnp.logical_not(r_same(h)))
            def _():
                r_copy(j, h).start()

    sigma = to_col(0.5 * jnp.exp(math.log(8.0) * step_in[...].astype(F32) / (NSTEPS - 1)))
    factor = 1.0 + (guide_scale - 1.0) * to_col(mask_in[...].astype(F32))

    def c_lanes(rr, qq, j):
        return pl.ds(pl.multiple_of(128 * (6 * rr + 3 * qq + j), 128), 128)

    def c_peer(n):
        return (c if n == 1 else 1 - c), (r if n == 0 else 1 - r)

    def c_copy(j, n):
        cc, rr = c_peer(n)
        lanes = c_lanes(r, c, j)
        return rcopy(cmb.at[:, lanes], cmb.at[:, lanes], sc.at[j, n], rc.at[j, n], dev(cc, x, k, y, rr))

    def c_wait(j, n):
        cc, rr = c_peer(n)
        lanes = c_lanes(rr, cc, j)
        rcopy(cmb.at[:, lanes], cmb.at[:, lanes], sc.at[j, n], rc.at[j, n], dev(cc, x, k, y, rr)).wait_recv()

    def combine(j):
        for b in range(2):
            rcopy(oz.at[b, j], oz.at[b, j], sr.at[j, 0], rz.at[b, j], dev(1 - c, x, k, y, r)).wait_recv()
        guided = factor * oz[0, j].astype(F32) + (1.0 - factor) * oz[1, j].astype(F32)
        cmb[:, c_lanes(r, c, j)] = guided.astype(BF16)
        for n in (1, 2, 0):
            c_copy(j, n).start()

    relay(0)
    w_first()
    relay(1)
    forward(0)
    w_rest()
    share(0)
    relay(2)

    forward(1)
    compute(0)
    share(1)
    forward(2)
    w_second()
    w_rest_z()
    compute(1)
    share(2)
    merge(0)
    compute(2)
    w_wait_b2()
    w_wait_a2()
    w_x(0)
    w_y(0)
    w_x(1)
    w_y(1)
    merge(1)
    combine(0)
    merge(2)
    combine(1)
    combine(2)
    for j in range(3):
        for n in range(3):
            c_wait(j, n)
    w_last()
    guided = dot_t(cmb[:, 0:384], wb[0].reshape(768, 384))
    for n in range(1, 4):
        guided += dot_t(cmb[:, 384 * n:384 * n + 384], wb[n].reshape(768, 384))
    out_ref[...] = (lat[...].astype(F32) - sigma * guided).astype(BF16)

    for j in range(3):
        for q in range(2):
            for t in range(3):
                copy, _src, _dst, _sem, same = z_remote(j, q, t)

                @pl.when(jnp.logical_not(same))
                def _():
                    copy.wait_send()

        for d in range(1, 4):
            x_copy(j, d, 0, 1).wait_send()
            y_copy(j, d, 0, 1).wait_send()
            o_copy(j, d).wait_send()
            l_copy(j, d).wait_send()
        for d in range(4):
            s_copy(j, d).wait_send()
        for h in range(2):
            @pl.when(jnp.logical_not(r_same(h)))
            def _():
                r_copy(j, h).wait_send()

        for n in range(3):
            c_copy(j, n).wait_send()

    @pl.when(jnp.logical_not(wself))
    def _():
        wcopy.wait_send()

    for d in range(1, 4):
        wz(d, k).wait_send()
        wc1(d, x).wait_send()
        wc2(d, y).wait_send()
        wc3(d, k).wait_send()
        wa2(d, y).wait_send()
        wb2(d, x).wait_send()
        for n in range(2):
            wa3(d, x, n).wait_send()
            wb3(d, y, n).wait_send()


def on_device(queries, keyvals, out_weight, latent, timestep, cond_mask):
    rows = queries.shape[1]
    dma = pltpu.SemaphoreType.DMA
    vmem = pltpu.VMEM
    anywhere = pl.BlockSpec(memory_space=pl.ANY)
    return pl.pallas_call(
        kernel,
        out_shape=jax.ShapeDtypeStruct((rows, 768), BF16),
        in_specs=[anywhere] * 4 + [pl.BlockSpec(memory_space=vmem)] * 2,
        out_specs=pl.BlockSpec(memory_space=vmem),
        scratch_shapes=[
            vmem((rows, 768), BF16),
            vmem((2, rows, 768), BF16),
            vmem((48, 768), BF16),
            vmem((rows, 768), BF16),
            vmem((2, 3, 4, 4, 128, HD), BF16),
            vmem((3, 4, 2, 128, HD), BF16),
            vmem((3, 4, 256, HD), BF16),
            vmem((3, 4, 256, HD), BF16),
            vmem((3, 4, 8, 128), F32),
            vmem((3, 4, 8, 128), F32),
            vmem((3, 2, 128, HD), BF16),
            vmem((2, 3, 128, HD), BF16),
            vmem((128, 1536), BF16),
            vmem((4, 4, 4, 48, 384), BF16),
            dma((3, 2, 3)), dma((3, 4)), dma((3, 4)), dma((3, 4)), dma((3, 4)), dma((3, 4)),
            dma((3, 2)), dma((3, 3)), dma((44,)),
            dma((3,)), dma((3,)), dma((3, 4)), dma((3, 4)), dma((3, 4)), dma((3, 4)), dma((3, 4)),
            dma((2, 3)), dma((3, 3)), dma, dma((10, 4)), dma((4,)),
        ],
        compiler_params=pltpu.CompilerParams(
            collective_id=0, has_side_effects=True, vmem_limit_bytes=58 << 20
        ),
    )(queries[0], keyvals[0], out_weight.T, latent, timestep.reshape(1, rows), cond_mask.reshape(1, rows))


def solution(mesh):
    placed = (
        P("cfg", "seq", "rep"),
        P("cfg", None, "seq", "rep"),
        P("rep", "seq"),
        P("seq", ("cfg", "rep")),
        P("seq"),
        P("seq"),
    )
    return jax.shard_map(
        on_device, mesh=mesh, in_specs=placed, out_specs=P("seq", ("cfg", "rep")), check_vma=False
    )
```
